32 devices in a mesh: qx: 8 (over z, y), qy: 4 (over x, core).
Axes of the slice: x: 2, y: 2, z: 4, core: 2. Of those that a mesh axis runs over, the one named last changes fastest.
Arguments:
- vectors: bfloat16 [64, 256, 512], P(None, 'qx', 'qy'), may hold values from -6 to 6
- near_tiles: bfloat16 [16, 32, 3, 256, 256], P('qx', 'qy'), may hold values from -0.21875 to 0.21875
- near_offset: int32 [16, 32, 3], P('qx', 'qy'), may hold values from 0 to 8, as said below
- col_basis: bfloat16 [16, 32, 64, 256], P('qx', 'qy'), may hold values from -0.375 to 0.375
- row_basis: bfloat16 [16, 32, 64, 256], P('qx', 'qy'), may hold values from -0.375 to 0.375
- up_transfer: float32 [16, 32, 64, 64], P('qx', 'qy'), may hold values from -0.375 to 0.375
- down_transfer: float32 [16, 32, 64, 64], P('qx', 'qy'), may hold values from -0.75 to 0.75
- coupling: float32 [32, 128, 64, 64], P(('qx', 'qy')), may hold values from -0.75 to 0.75
- couple_dest: int32 [32, 128], replicated, may hold values from -1 to 31, as said below
- couple_target: int32 [32, 128], replicated, may hold values from 0 to 19, as said below
Outputs:
- product: float32 [64, 256, 512], P(None, 'qx', 'qy')
The draws below stay inside these ranges and needn't reach their ends.
Inputs may be any that keep to these rules, and one draw needn't show every extreme that they name: `couple_dest`: in each row (source device) no destination device appears more than 4 times; in every draw one destination device appears exactly 4 times in every row; -1 marks a padded slot. `couple_target`: slots below 96 name a leaf cluster (0 to 15), the others a parent cluster (16 to 19) of the target device. `near_offset`: the 3 codes of a leaf are distinct; code o reads the leaf at offset (o // 3 - 1, o % 3 - 1).
All inputs are finite; a program needn't handle non-finite values.
Results may differ from the reference program's by a relative error of at most 0.0003.
Values may be sent and summed in bfloat16 or wider, within the bound.
A program may use at most 64 MiB of HBM per device.

```python
import jax
import jax.numpy as jnp
from jax import lax

R = 64
VECS = 64
LS = 16
NEAR = 3
K0 = 6
K1 = 8
CY = 128
LP = 256
LEAVES_DEV = 16
L1_DEV = 4
CLUSTERS = 20
SLOTS = 128
CAP = 4
NX = 256
NY = 512
GX = 16
GY = 32
N_QX = 8
N_QY = 4
DEVICES = 32


def draw_couple_dest(key, part):
    key = jax.random.fold_in(key, 101)
    key_hot, key_order, key_shuffle, key_live = jax.random.split(key, 4)
    total = DEVICES * CAP
    hot_device = jax.random.randint(key_hot, (), 0, DEVICES)
    ident = jnp.arange(total, dtype=jnp.int32)
    owner = ident // CAP
    scores = jax.random.randint(key_order, (DEVICES, total), 0, 1 << 20) * total + ident[None, :]
    scores = jnp.where(owner[None, :] == hot_device, ident[None, :] - total, scores)
    chosen = jnp.argsort(scores, axis=1)[:, :SLOTS].astype(jnp.int32)
    dest = chosen // CAP
    slot_ident = jnp.arange(SLOTS, dtype=jnp.int32)
    shuffle = jnp.argsort(jax.random.randint(key_shuffle, (DEVICES, SLOTS), 0, 1 << 20) * SLOTS + slot_ident[None, :], axis=1).astype(jnp.int32)
    dest = jnp.take_along_axis(dest, shuffle, axis=1)
    live = (jax.random.randint(key_live, (DEVICES, SLOTS), 0, 20) >= 3) | (dest == hot_device)
    return jnp.where(live, dest, -1).astype(jnp.int32)


def draw_couple_target(key, part):
    key = jax.random.fold_in(key, 202)
    drawn = jax.random.randint(key, (DEVICES, SLOTS), 0, 1 << 20)
    column = jnp.arange(SLOTS, dtype=jnp.int32)[None, :]
    leaf_part = column < LEAVES_DEV * K0
    return jnp.where(leaf_part, drawn % LEAVES_DEV, LEAVES_DEV + drawn % L1_DEV).astype(jnp.int32)


def draw_near_offset(key, part):
    key = jax.random.fold_in(key, 303)
    scores = jax.random.randint(key, (GX, GY, 9), 0, 1 << 20) * 9 + jnp.arange(9, dtype=jnp.int32)
    return jnp.argsort(scores, axis=2)[:, :, :NEAR].astype(jnp.int32)


def levels(own_key, extent, cuts, low, largest):
    gain = 1.0
    for position, blocks in cuts:
        draws = jax.random.uniform(jax.random.fold_in(jax.random.fold_in(own_key, 6), position), (blocks,), jnp.float32, low / len(cuts), largest / len(cuts))
        gain = gain * jnp.repeat(jnp.exp(draws), extent[position] // blocks).reshape((-1,) + (1,) * (len(extent) - 1 - position))
    return gain


def bell_draw(own_key, dims, deviation, bound, cuts=(), kind=jnp.bfloat16):
    values = jax.random.normal(own_key, dims, jnp.float32) * deviation
    if len(cuts) > 0:
        values = levels(own_key, dims, cuts, -0.22, 0.18) * values
    return jnp.clip(values, min=-bound, max=bound).astype(kind)


def setup_inputs(seed: int = 0) -> dict:
    key_list = jax.random.split(jax.random.key(seed), 11)
    vectors = bell_draw(key_list[0], (VECS, NX, NY), 1.0, 6.0, ((1, 8), (2, 4)))
    near_tiles = bell_draw(key_list[1], (GX, GY, NEAR, LP, LP), (NEAR * LP) ** -0.5, 0.21875, ((0, 8), (1, 4)))
    near_offset = draw_near_offset(jax.random.fold_in(key_list[10], 71), 0)
    col_basis = bell_draw(key_list[3], (GX, GY, R, LP), LP ** -0.5, 0.375, ((0, 8), (1, 4)))
    row_basis = bell_draw(key_list[4], (GX, GY, R, LP), LP ** -0.5, 0.375, ((0, 8), (1, 4)))
    up_transfer = bell_draw(key_list[5], (GX, GY, R, R), (4 * R) ** -0.5, 0.375, ((0, 8), (1, 4)), jnp.float32)
    down_transfer = bell_draw(key_list[6], (GX, GY, R, R), R ** -0.5, 0.75, ((0, 8), (1, 4)), jnp.float32)
    coupling = bell_draw(key_list[7], (DEVICES, SLOTS, R, R), R ** -0.5, 0.75, ((0, 32),), jnp.float32)
    couple_dest = draw_couple_dest(jax.random.fold_in(key_list[10], 71), 0)
    couple_target = draw_couple_target(jax.random.fold_in(key_list[10], 71), 0)
    return dict(vectors=vectors, near_tiles=near_tiles, near_offset=near_offset, col_basis=col_basis, row_basis=row_basis, up_transfer=up_transfer, down_transfer=down_transfer, coupling=coupling, couple_dest=couple_dest, couple_target=couple_target)


def reference(vectors, near_tiles, near_offset, col_basis, row_basis, up_transfer, down_transfer, coupling, couple_dest, couple_target):
    precise = lax.Precision.HIGHEST
    grid_x = NX // LS
    grid_y = NY // LS
    leaf_y = CY // LS
    devices = N_QX * N_QY
    blocks = vectors.reshape(VECS, grid_x, LS, grid_y, LS).transpose(1, 3, 0, 2, 4).reshape(grid_x, grid_y, VECS, LP)
    leaf_coef = jnp.einsum('ijrp,ijvp->ijrv', col_basis.astype(jnp.float32), blocks.astype(jnp.float32), precision=precise)
    lifted = jnp.einsum('ijrs,ijsv->ijrv', up_transfer, leaf_coef, precision=precise)
    upper_coef = lifted.reshape(grid_x // 2, 2, grid_y // 2, 2, R, VECS).sum(axis=(1, 3))
    leaf_dev = leaf_coef.reshape(N_QX, 2, N_QY, leaf_y, R, VECS).transpose(0, 2, 1, 3, 4, 5).reshape(devices, LEAVES_DEV, R, VECS)
    upper_dev = upper_coef.reshape(N_QX, N_QY, L1_DEV, R, VECS).reshape(devices, L1_DEV, R, VECS)

    def send_step(totals, device_item):
        leaf_part, upper_part, couple_block, dest_row, target_row = device_item
        source_coef = jnp.concatenate([jnp.repeat(leaf_part, K0, axis=0), jnp.repeat(upper_part, K1, axis=0)], axis=0)
        contrib = jnp.einsum('srt,stv->srv', couple_block, source_coef, precision=precise).reshape(SLOTS, R * VECS)
        segment_ids = jnp.where(dest_row >= 0, dest_row * CLUSTERS + target_row, devices * CLUSTERS).astype(jnp.int32)
        return totals.at[segment_ids].add(contrib), None

    totals = jnp.zeros((devices * CLUSTERS + 1, R * VECS), jnp.float32)
    totals, _ = lax.scan(send_step, totals, (leaf_dev, upper_dev, coupling, couple_dest, couple_target))
    gathered = totals[:devices * CLUSTERS].reshape(devices, CLUSTERS, R, VECS)
    down_leaf = gathered[:, :LEAVES_DEV].reshape(N_QX, N_QY, 2, leaf_y, R, VECS).transpose(0, 2, 1, 3, 4, 5).reshape(grid_x, grid_y, R, VECS)
    down_upper = gathered[:, LEAVES_DEV:].reshape(N_QX, N_QY * L1_DEV, R, VECS)
    expanded = jnp.repeat(jnp.repeat(down_upper, 2, axis=0), 2, axis=1)
    down_leaf = down_leaf + jnp.einsum('ijrs,ijsv->ijrv', down_transfer, expanded, precision=precise)
    far_out = jnp.einsum('ijrp,ijrv->ijvp', row_basis.astype(jnp.float32), down_leaf, precision=precise)

    padded = jnp.pad(vectors, ((0, 0), (LS, LS), (LS, LS)))
    padded_blocks = padded.reshape(VECS, grid_x + 2, LS, grid_y + 2, LS).transpose(1, 3, 0, 2, 4).reshape((grid_x + 2) * (grid_y + 2), VECS, LP)
    along_x = jnp.arange(grid_x, dtype=jnp.int32)[:, None, None]
    along_y = jnp.arange(grid_y, dtype=jnp.int32)[None, :, None]
    tile_index = ((along_x + near_offset // 3) * (grid_y + 2) + along_y + near_offset % 3).astype(jnp.int32)

    def near_row(leaf_row):
        tiles = near_tiles[leaf_row].astype(jnp.float32)
        picked = padded_blocks[tile_index[leaf_row]].astype(jnp.float32)
        return jnp.einsum('jkps,jkvs->jvp', tiles, picked, precision=precise)

    near_out = lax.map(near_row, jnp.arange(grid_x, dtype=jnp.int32))
    total_out = near_out + far_out
    return total_out.reshape(grid_x, grid_y, VECS, LS, LS).transpose(2, 0, 3, 1, 4).reshape(VECS, NX, NY)
```

```python
import jax
import jax.numpy as jnp
from jax import lax
from jax.experimental import pallas as pl
from jax.experimental.pallas import tpu as pltpu
from jax.sharding import PartitionSpec as P

LS = 16
K0 = 6
K1 = 8
TOP = 15
LANES = 128

ANY = pl.BlockSpec(memory_space=pl.ANY)
VM = pl.BlockSpec(memory_space=pltpu.VMEM)
SM = pl.BlockSpec(memory_space=pltpu.SMEM)
MESH = pl.DeviceIdType.MESH
F32 = jnp.float32
BF16 = jnp.bfloat16
STEPS = [(1, 0), (-1, 0), (0, 1), (0, -1), (1, 1), (1, -1), (-1, 1), (-1, -1)]


def halves(value):
    high = value.astype(BF16)
    return high, (value - high.astype(F32)).astype(BF16)


def product_of(left, right):
    lh, ll = halves(left)
    rh, rl = halves(right)
    return jnp.dot(
        jnp.concatenate([lh, ll, lh, ll], axis=1),
        jnp.concatenate([rh, rh, rl, rl], axis=0),
        preferred_element_type=F32,
    )


def unfolded(value):
    half = value.shape[1] // 2
    return jnp.concatenate([value[:, :half], value[:, half:]], axis=0)


def first_kernel(
    leaf_x,
    leaf_y,
    capacity,
    off_ref,
    dest_any,
    tgt_any,
    vec_any,
    col_any,
    up_any,
    coup_any,
    tiles_any,
    recv_ref,
    rscale_ref,
    near_ref,
    land_ref,
    dest_v,
    tgt_v,
    vec_v,
    col_v,
    up_v,
    coup_v,
    tiles_v,
    vec_f,
    slot_v,
    slot_s,
    coef,
    rhs,
    mats,
    blocks,
    outgo,
    oscale,
    full,
    load_sem,
    tile_sem,
    halo_send,
    halo_recv,
    data_send,
    data_recv,
    scale_send,
    scale_recv,
):
    width_x = lax.axis_size("qx")
    width_y = lax.axis_size("qy")
    devices = width_x * width_y
    here_x = lax.axis_index("qx")
    here_y = lax.axis_index("qy")
    me = here_x * width_y + here_y
    leaf_count = leaf_x * leaf_y
    upper_count = leaf_y // 2
    cluster_count = leaf_count + upper_count
    slot_count = coup_v.shape[2]
    rank = coup_v.shape[0]
    half = rank // 2
    vecs = vec_v.shape[0]
    rows_y = vec_v.shape[2]
    near_count = tiles_v.shape[1]
    pairs = LS // 2
    wide = leaf_y + 2
    i32 = jnp.int32

    loads = [
        pltpu.make_async_copy(src, dst, load_sem.at[n])
        for n, (src, dst) in enumerate(
            (
                (dest_any, dest_v),
                (vec_any, vec_v),
                (col_any, col_v),
                (up_any, up_v),
                (coup_any, coup_v),
                (tgt_any, tgt_v),
            )
        )
    ]
    for load in loads:
        load.start()

    def tile_load(m):
        return pltpu.make_async_copy(tiles_any.at[m], tiles_v.at[m], tile_sem.at[m])

    def peer_of(t):
        u = t // width_y
        turn = lax.rem(u + 1, 2) * -u // 2 + lax.rem(u, 2) * ((u + 1) // 2)
        x = lax.rem(here_x + width_x // 2 + turn + width_x, width_x)
        y = lax.rem(here_y + t + 1, width_y)
        return x, y

    def source_of(t):
        u = t // width_y
        turn = lax.rem(u + 1, 2) * -u // 2 + lax.rem(u, 2) * ((u + 1) // 2)
        x = lax.rem(here_x - width_x // 2 - turn + 2 * width_x, width_x)
        y = lax.rem(here_y - lax.rem(t + 1, width_y) + width_y, width_y)
        return x, y

    barrier = pltpu.get_barrier_semaphore()

    def greet(t, carry):
        pl.semaphore_signal(barrier, inc=1, device_id=peer_of(t), device_id_type=MESH)
        return carry

    lax.fori_loop(0, devices - 1, greet, 0)

    loads[0].wait()
    places = devices * capacity
    own_row = jnp.broadcast_to(dest_v[pl.ds(me, 1), :], (slot_count, slot_count))
    own_col = own_row.T
    ident_row = lax.broadcasted_iota(i32, (slot_count, slot_count), 1)
    ident_col = lax.broadcasted_iota(i32, (slot_count, slot_count), 0)
    before = (own_row == own_col) & (ident_row < ident_col)
    order = jnp.sum(before.astype(F32), axis=1, keepdims=True).astype(i32)
    position = jnp.where(own_col[:, :1] >= 0, own_col[:, :1] * capacity + order, places)
    place = lax.broadcasted_iota(i32, (slot_count, places), 1)
    ident = lax.broadcasted_iota(i32, (slot_count, places), 0)
    chosen = jnp.where(position == place, (ident - slot_count).astype(F32), 0.0)
    slot_v[...] = slot_count + jnp.sum(chosen, axis=0, keepdims=True).astype(i32)

    loads[1].wait()
    vec_f[...] = vec_v[...].astype(F32)

    def block_step(n, carry):
        i = n // pairs
        x = lax.rem(n, pairs)
        first = vec_f[:, i * LS + x, :]
        second = vec_f[:, i * LS + x + pairs, :]
        both = jnp.concatenate([first, second], axis=0).T.astype(BF16)
        for j in range(leaf_y):
            blocks[(i + 1) * wide + j + 1, pl.ds(pl.multiple_of(x * LS, LS), LS), :] = both[j * LS : (j + 1) * LS]
        return carry

    lax.fori_loop(0, leaf_x * pairs, block_step, 0, unroll=2)

    slot_copy = pltpu.make_async_copy(slot_v, slot_s, load_sem.at[len(loads)])
    slot_copy.start()

    def present(dx, dy):
        x = here_x + dx
        y = here_y + dy
        return (x >= 0) & (x < width_x) & (y >= 0) & (y < width_y)

    def halo_spans(dx, dy):
        rows = [1 if dx <= 0 else leaf_x] if dx != 0 else list(range(1, leaf_x + 1))
        land = [0 if dx > 0 else leaf_x + 1] if dx != 0 else rows
        count = leaf_y if dy == 0 else 1
        col = 1 if dy <= 0 else leaf_y
        to = 1 if dy == 0 else (0 if dy > 0 else leaf_y + 1)
        return [(r * wide + col, w * wide + to, count) for r, w in zip(rows, land)]

    def halo_copies(n):
        dx, dy = STEPS[n]
        out = []
        for q, (src, dst, count) in enumerate(halo_spans(dx, dy)):
            out.append(
                pltpu.make_async_remote_copy(
                    src_ref=blocks.at[pl.ds(src, count)],
                    dst_ref=blocks.at[pl.ds(dst, count)],
                    send_sem=halo_send.at[n, q],
                    recv_sem=halo_recv.at[n, q],
                    device_id=(here_x + dx, here_y + dy),
                    device_id_type=MESH,
                )
            )
        return out

    for dx, dy in STEPS:

        @pl.when(jnp.logical_not(present(-dx, -dy)))
        def _():
            for _, dst, count in halo_spans(dx, dy):
                blocks[pl.ds(dst, count)] = jnp.zeros((count,) + blocks.shape[1:], BF16)

    pl.semaphore_wait(barrier, devices - 1)
    for n, (dx, dy) in enumerate(STEPS):

        @pl.when(present(dx, dy))
        def _():
            for copy in halo_copies(n):
                copy.start()

    loads[2].wait()
    diag_zero = jnp.zeros((rank, vecs), BF16)

    def keep(m, value):
        coef[m] = value
        high, low = halves(value)
        top = jnp.concatenate([high, diag_zero, low, diag_zero], axis=1)
        bottom = jnp.concatenate([diag_zero, high, diag_zero, low], axis=1)
        rhs[m] = jnp.concatenate([top, bottom, top, bottom], axis=0)

    def leaf_step(m, carry):
        i = m // leaf_y
        j = lax.rem(m, leaf_y)
        block = unfolded(blocks[(i + 1) * wide + j + 1])
        keep(m, jnp.dot(col_v[m], block, preferred_element_type=F32))
        return carry

    lax.fori_loop(0, leaf_count, leaf_step, 0, unroll=4)
    loads[3].wait()

    def upper_step(p, carry):
        total = None
        for i in range(leaf_x):
            for c in range(2):
                m = i * leaf_y + 2 * p + c
                term = product_of(up_v[m], coef[m])
                total = term if total is None else total + term
        keep(leaf_count + p, total)
        return carry

    lax.fori_loop(0, upper_count, upper_step, 0, unroll=2)

    loads[4].wait()
    for m in range(leaf_count):
        tile_load(m).start()

    def turn_step(r, carry):
        mats[0:slot_count, r, :] = jnp.concatenate([coup_v[r], coup_v[r + half]], axis=0).T
        return carry

    mats[slot_count] = jnp.zeros((half, 2 * rank), F32)
    lax.fori_loop(0, half, turn_step, 0, unroll=2)
    slot_copy.wait()

    def data_copy(t, dst, device):
        return pltpu.make_async_remote_copy(
            src_ref=outgo.at[t],
            dst_ref=recv_ref.at[dst],
            send_sem=data_send.at[t],
            recv_sem=data_recv.at[dst],
            device_id=device,
            device_id_type=MESH,
        )

    def scale_copy(t, dst, device):
        return pltpu.make_async_remote_copy(
            src_ref=oscale.at[t],
            dst_ref=rscale_ref.at[dst],
            send_sem=scale_send.at[t],
            recv_sem=scale_recv.at[dst],
            device_id=device,
            device_id_type=MESH,
        )

    def contribution(p):
        s = jnp.clip(slot_s[0, p], 0, slot_count)
        upper = leaf_count + (s - leaf_count * K0) // K1
        m = jnp.clip(jnp.where(s < leaf_count * K0, s // K0, upper), 0, cluster_count - 1)
        high, low = halves(mats[s])
        res = jnp.dot(jnp.concatenate([high, low], axis=1), rhs[m], preferred_element_type=F32)
        return res[:, : 2 * vecs] + res[:, 2 * vecs :]

    def fill(t):
        x, y = peer_of(t)
        first = (x * width_y + y) * capacity
        values = [contribution(first + k) for k in range(capacity)]
        peak = None
        for value in values:
            size = jnp.abs(value)
            peak = size if peak is None else jnp.maximum(peak, size)
        peak = jnp.max(peak, axis=0, keepdims=True)
        power = jnp.ceil(jnp.log2(jnp.maximum(peak, 1e-30)))
        grow = jnp.exp2(TOP - power)
        oscale[t] = jnp.exp2(power - TOP)
        limit = 2.0**TOP - 1
        for k, value in enumerate(values):
            whole = jnp.clip(jnp.round(value * grow), -limit, limit)
            outgo[t, k * half : (k + 1) * half, :] = whole.astype(i32).astype(jnp.int16)

    def send(t):
        data_copy(t, me, peer_of(t)).start()
        scale_copy(t, me, peer_of(t)).start()

    def dest_step(t, carry):
        fill(t)

        @pl.when(t > 0)
        def _():
            send(t - 1)

        return carry

    lax.fori_loop(0, devices, dest_step, 0, unroll=2)
    own = [
        pltpu.make_async_copy(outgo.at[devices - 1], recv_ref.at[me], data_recv.at[me]),
        pltpu.make_async_copy(oscale.at[devices - 1], rscale_ref.at[me], scale_recv.at[me]),
    ]

    loads[5].wait()
    hits = dest_v[...] == me
    upto = (ident_col < ident_row).astype(BF16)
    ahead = jnp.dot(hits.astype(F32).astype(BF16), upto, preferred_element_type=F32).astype(i32)
    lane = lax.broadcasted_iota(i32, (devices, LANES), 1)
    landing = jnp.zeros((devices, LANES), F32)
    for k in range(capacity):
        taken = jnp.where(hits & (ahead == k), (tgt_v[...] - cluster_count).astype(F32), 0.0)
        landing = jnp.where(lane == k, jnp.sum(taken, axis=1, keepdims=True), landing)
    land_ref[...] = cluster_count + landing.astype(i32)
    for copy in own:
        copy.start()

    for n, (dx, dy) in enumerate(STEPS):

        @pl.when(present(-dx, -dy))
        def _():
            for copy in halo_copies(n):
                copy.wait_recv()

    def near_step(m, carry):
        tile_load(m).wait()
        i = m // leaf_y
        j = lax.rem(m, leaf_y)
        total = None
        for k in range(near_count):
            o = off_ref[m, k]
            block = unfolded(blocks[(i + o // 3) * wide + j + lax.rem(o, 3)])
            term = jnp.dot(tiles_v[m, k], block, preferred_element_type=F32)
            total = term if total is None else total + term
        full[m] = total
        return carry

    lax.fori_loop(0, leaf_count, near_step, 0, unroll=2)
    for i in range(leaf_x):
        for x in range(LS):
            rows = [full[i * leaf_y + j, x * LS : (x + 1) * LS, :] for j in range(leaf_y)]
            near_ref[:, i * LS + x, :] = jnp.concatenate(rows, axis=0).T

    for n, (dx, dy) in enumerate(STEPS):

        @pl.when(present(dx, dy))
        def _():
            for copy in halo_copies(n):
                copy.wait_send()

    def finish(t, carry):
        x, y = source_of(t)
        src = x * width_y + y
        data_copy(t, src, (x, y)).wait_recv()
        scale_copy(t, src, (x, y)).wait_recv()
        data_copy(t, me, peer_of(t)).wait_send()
        scale_copy(t, me, peer_of(t)).wait_send()
        return carry

    lax.fori_loop(0, devices - 1, finish, 0)
    for copy in own:
        copy.wait()


def far_kernel(leaf_x, leaf_y, capacity, land_ref, recv_ref, rscale_ref, down_ref, row_ref, near_ref, out_ref, acc, full):
    leaf_count = leaf_x * leaf_y
    half = acc.shape[1]
    acc[...] = jnp.zeros_like(acc)

    def add(src, carry):
        scale = rscale_ref[src]
        for k in range(capacity):
            t = land_ref[src, k]
            acc[t] = acc[t] + recv_ref[src, k * half : (k + 1) * half, :].astype(F32) * scale
        return carry

    lax.fori_loop(0, recv_ref.shape[0], add, 0, unroll=2)

    def leaf(m, carry):
        j = lax.rem(m, leaf_y)
        value = unfolded(acc[m]) + product_of(down_ref[m], unfolded(acc[leaf_count + j // 2]))
        high, low = halves(value)
        basis = row_ref[m]
        full[m] = lax.dot_general(
            jnp.concatenate([basis, basis], axis=0),
            jnp.concatenate([high, low], axis=0),
            (((0,), (0,)), ((), ())),
            preferred_element_type=F32,
        )
        return carry

    lax.fori_loop(0, leaf_count, leaf, 0, unroll=4)
    for a in range(leaf_x):
        for i in range(LS):
            rows = [full[a * leaf_y + h, i * LS : (i + 1) * LS, :] for h in range(leaf_y)]
            x = a * LS + i
            out_ref[:, x, :] = near_ref[:, x, :] + jnp.concatenate(rows, axis=0).T


def body(
    vectors,
    near_tiles,
    near_offset,
    col_basis,
    row_basis,
    up_transfer,
    down_transfer,
    coupling,
    couple_dest,
    couple_target,
):
    shape = jax.ShapeDtypeStruct
    devices = lax.axis_size("qx") * lax.axis_size("qy")
    vec_count, rows_x, rows_y = vectors.shape
    leaf_x = rows_x // LS
    leaf_y = rows_y // LS
    leaf_count = leaf_x * leaf_y
    cluster_count = leaf_count + leaf_y // 2
    rank = coupling.shape[2]
    slot_count = coupling.shape[1]
    capacity = (slot_count + devices - 1) // devices
    near_count = near_tiles.shape[2]
    points = LS * LS
    half = rank // 2
    block = (points // 2, 2 * vec_count)
    dma = pltpu.SemaphoreType.DMA

    recv, rscale, near, land = pl.pallas_call(
        lambda *refs: first_kernel(leaf_x, leaf_y, capacity, *refs),
        out_shape=(
            shape((devices, capacity * half, 2 * vec_count), jnp.int16),
            shape((devices, 1, 2 * vec_count), F32),
            shape((vec_count, rows_x, rows_y), F32),
            shape((devices, LANES), jnp.int32),
        ),
        in_specs=[SM] + [ANY] * 7,
        out_specs=(ANY, ANY, VM, VM),
        scratch_shapes=[
            pltpu.VMEM(couple_dest.shape, jnp.int32),
            pltpu.VMEM(couple_target.shape, jnp.int32),
            pltpu.VMEM(vectors.shape, BF16),
            pltpu.VMEM((leaf_count, rank, points), BF16),
            pltpu.VMEM((leaf_count, rank, rank), F32),
            pltpu.VMEM((rank, rank, slot_count), F32),
            pltpu.VMEM((leaf_count, near_count, points, points), BF16),
            pltpu.VMEM(vectors.shape, F32),
            pltpu.VMEM((1, devices * capacity), jnp.int32),
            pltpu.SMEM((1, devices * capacity), jnp.int32),
            pltpu.VMEM((cluster_count, rank, vec_count), F32),
            pltpu.VMEM((cluster_count, 4 * rank, 4 * vec_count), BF16),
            pltpu.VMEM((slot_count + 1, half, 2 * rank), F32),
            pltpu.VMEM(((leaf_x + 2) * (leaf_y + 2),) + block, BF16),
            pltpu.VMEM((devices, capacity * half, 2 * vec_count), jnp.int16),
            pltpu.VMEM((devices, 1, 2 * vec_count), F32),
            pltpu.VMEM((leaf_count, points, vec_count), F32),
            dma((7,)),
            dma((leaf_count,)),
            dma((len(STEPS), leaf_x)),
            dma((len(STEPS), leaf_x)),
            dma((devices,)),
            dma((devices,)),
            dma((devices,)),
            dma((devices,)),
        ],
        compiler_params=pltpu.CompilerParams(collective_id=0, has_side_effects=True),
        name="send",
    )(
        near_offset.reshape(leaf_count, near_count),
        couple_dest,
        couple_target,
        vectors,
        col_basis.reshape(leaf_count, rank, points),
        up_transfer.reshape(leaf_count, rank, rank),
        coupling[0].transpose(1, 2, 0),
        near_tiles.reshape(leaf_count, near_count, points, points),
    )

    return pl.pallas_call(
        lambda *refs: far_kernel(leaf_x, leaf_y, capacity, *refs),
        out_shape=shape((vec_count, rows_x, rows_y), F32),
        in_specs=[SM, VM, VM, VM, VM, VM],
        out_specs=VM,
        scratch_shapes=[
            pltpu.VMEM((cluster_count + 1, half, 2 * vec_count), F32),
            pltpu.VMEM((leaf_count, points, vec_count), F32),
        ],
        name="far",
    )(
        land,
        recv,
        rscale,
        down_transfer.reshape(leaf_count, rank, rank),
        row_basis.reshape(leaf_count, rank, points),
        near,
    )


def solution(mesh):
    return jax.shard_map(
        body,
        mesh=mesh,
        in_specs=(
            P(None, "qx", "qy"),
            P("qx", "qy", None, None, None),
            P("qx", "qy", None),
            P("qx", "qy", None, None),
            P("qx", "qy", None, None),
            P("qx", "qy", None, None),
            P("qx", "qy", None, None),
            P(("qx", "qy"), None, None, None),
            P(),
            P(),
        ),
        out_specs=P(None, "qx", "qy"),
        check_vma=False,
    )
```
